32 devices in a mesh: ctx: 8 (over y, x, core), fsdp: 4 (over z).
Axes of the slice: x: 2, y: 2, z: 4, core: 2. Of those that a mesh axis runs over, the one named last changes fastest.
Arguments:
- queries: bfloat16 [4096, 8192], P('ctx', 'fsdp'), may hold values from -1.796875 to 1.796875
- keys: bfloat16 [4096, 8192], P('ctx', 'fsdp'), may hold values from -1.796875 to 1.796875
- values: bfloat16 [4096, 8192], P('ctx', 'fsdp'), may hold values from -18 to 18
- grad_out: bfloat16 [4096, 8192], P('ctx', 'fsdp'), may hold values from -18 to 18
- log_decay: float32 [4096, 64], P('ctx', 'fsdp'), may hold values from -1 to 0
- gain: float32 [8192], P('fsdp'), may hold values from 0.5 to 1.5
Outputs:
- grad_queries: bfloat16 [4096, 8192], P('ctx', 'fsdp')
- grad_keys: bfloat16 [4096, 8192], P('ctx', 'fsdp')
- grad_values: bfloat16 [4096, 8192], P('ctx', 'fsdp')
- grad_gain: float32 [8192], P('fsdp')
The draws below stay inside these ranges and needn't reach their ends.
All inputs are finite; a program needn't handle non-finite values.
Results may differ from the reference program's by a relative error of at most 0.001.
Values sent between devices are 32-bit elements; how exact they have to be, the bound alone decides.
A program may use at most 128 MiB of HBM per device.

```python
import jax
import jax.numpy as jnp
from jax import lax

HEAD_TOTAL = 64
HDIM = 128
TOK_DEV = 512
HD = 8192
SEQUENCE_LENGTH = 4096
N_CTX = 8


def draw_log_decay(key, part):
    every_key_row = jax.random.split(key, 7)
    fast_share = 0.5
    fast_heads = jax.random.uniform(every_key_row[0], (HEAD_TOTAL,)) < fast_share
    fast_rate = jnp.exp(jax.random.uniform(every_key_row[1], (HEAD_TOTAL,), minval=jnp.log(0.03), maxval=jnp.log(0.1)))
    slow_rate = jnp.exp(jax.random.uniform(every_key_row[2], (HEAD_TOTAL,), minval=jnp.log(0.05), maxval=jnp.log(0.3))) / SEQUENCE_LENGTH
    baseline_decay_rate = jnp.where(fast_heads, fast_rate, slow_rate)
    jitter_level = jax.random.uniform(every_key_row[3], (SEQUENCE_LENGTH, HEAD_TOTAL), minval=0.4, maxval=1.6)
    partition_multiplier = jnp.exp(jax.random.uniform(every_key_row[4], (SEQUENCE_LENGTH // TOK_DEV, 1, HEAD_TOTAL), minval=jnp.log(0.5), maxval=jnp.log(2.0)))
    partition_multiplier = jnp.broadcast_to(partition_multiplier, (SEQUENCE_LENGTH // TOK_DEV, TOK_DEV, HEAD_TOTAL)).reshape(SEQUENCE_LENGTH, HEAD_TOTAL)
    spike_enabled = jax.random.uniform(every_key_row[5], (SEQUENCE_LENGTH, HEAD_TOTAL)) < 2.0 / SEQUENCE_LENGTH
    spike_magnitude = jax.random.uniform(every_key_row[6], (SEQUENCE_LENGTH, HEAD_TOTAL), minval=0.22, maxval=0.51)
    return -(baseline_decay_rate[None, :] * jitter_level * partition_multiplier + jnp.where(spike_enabled, spike_magnitude, 0.0))


def draw_grad_out(key, part):
    pieces = jax.random.split(key, 1)
    position = jnp.arange(SEQUENCE_LENGTH, dtype=jnp.float32)[:, None] / max(SEQUENCE_LENGTH - 1, 1)
    feature = jnp.arange(HD, dtype=jnp.float32)[None, :] / max(HD - 1, 1)
    scaling = (1.0 + 2.0 * position) * (1.0 + feature)
    return (jnp.clip(jax.random.normal(pieces[0], (SEQUENCE_LENGTH, HD)), -3.0, 3.0) * scaling).astype(jnp.bfloat16)


def draw_values(key, part):
    pieces = jax.random.split(key, 1)
    feature = jnp.arange(HD, dtype=jnp.float32)[None, :] / max(HD - 1, 1)
    scaling = 1.0 + 2.0 * feature
    return (jnp.clip(jax.random.normal(pieces[0], (SEQUENCE_LENGTH, HD)), -5.0, 5.0) * scaling).astype(jnp.bfloat16)


def block_levels(stream_key, dims, cuts, low, high):
    def one(dim, shards_of):
        heights = jax.random.uniform(jax.random.fold_in(jax.random.fold_in(stream_key, 6), dim), (shards_of,), jnp.float32, low / len(cuts), high / len(cuts))
        return jnp.repeat(jnp.exp(heights), dims[dim] // shards_of).reshape((-1,) + (1,) * (len(dims) - dim - 1))

    level = one(*cuts[0])
    for cut in cuts[1:]:
        level = level * one(*cut)
    return level


def gaussian(stream_key, extent, deviation, reach, cuts=(), kind=jnp.bfloat16):
    array = deviation * jax.random.normal(stream_key, extent, jnp.float32)
    if cuts:
        array = array * block_levels(stream_key, extent, cuts, -0.22, 0.18)
    return jnp.clip(array, -reach, reach).astype(kind)


def setup_inputs(seed: int = 0) -> dict:
    splits = jax.random.split(jax.random.key(seed), 7)
    queries = gaussian(splits[0], (SEQUENCE_LENGTH, HD), 0.3, 1.796875, ((0, 8), (1, 4)))
    keys = gaussian(splits[1], (SEQUENCE_LENGTH, HD), 0.3, 1.796875, ((0, 8), (1, 4)))
    values = draw_values(jax.random.fold_in(splits[6], 71), 0)
    grad_out = draw_grad_out(jax.random.fold_in(splits[6], 71), 0)
    log_decay = draw_log_decay(jax.random.fold_in(splits[6], 71), 0)
    gain = jnp.clip(1.0 + 0.1 * jax.random.normal(splits[5], (HD,), jnp.float32), 0.5, 1.5)
    return dict(queries=queries, keys=keys, values=values, grad_out=grad_out, log_decay=log_decay, gain=gain)


HIGHEST = lax.Precision.HIGHEST
epsilon = 1e-06

def to_blocks(array_in):
    return array_in.astype(jnp.float32).reshape(N_CTX, TOK_DEV, HEAD_TOTAL, HDIM).transpose(0, 2, 1, 3)

def from_blocks(array_in):
    return array_in.transpose(0, 2, 1, 3).reshape(SEQUENCE_LENGTH, HD)

def decay_weights(log_prefix):
    row_count = log_prefix.shape[-1]
    lower = jnp.arange(row_count)[:, None] >= jnp.arange(row_count)[None, :]
    spread = log_prefix[..., :, None] - log_prefix[..., None, :]
    return jnp.where(lower, jnp.exp(jnp.where(lower, spread, 0.0)), 0.0)

def reference(queries, keys, values, grad_out, log_decay, gain):
    query_heads = to_blocks(queries)
    key_heads = to_blocks(keys)
    value_heads = to_blocks(values)
    log_prefix = jnp.cumsum(log_decay.reshape(N_CTX, TOK_DEV, HEAD_TOTAL), axis=1).transpose(0, 2, 1)
    log_total = log_prefix[..., -1]

    def forward_step(kv_state, block_item):
        query_b, key_b, value_b, prefix_b, total_b = block_item
        weights = decay_weights(prefix_b)
        score_masked = jnp.einsum('hte,hse->hts', query_b, key_b, precision=HIGHEST) * weights
        attended = jnp.einsum('hts,hse->hte', score_masked, value_b, precision=HIGHEST)
        attended = attended + jnp.exp(prefix_b)[..., None] * jnp.einsum('hte,hef->htf', query_b, kv_state, precision=HIGHEST)
        key_scaled = key_b * jnp.exp(total_b[:, None] - prefix_b)[..., None]
        new_state = jnp.exp(total_b)[:, None, None] * kv_state + jnp.einsum('hse,hsf->hef', key_scaled, value_b, precision=HIGHEST)
        return (new_state, (attended, kv_state))
    zero_state = jnp.zeros((HEAD_TOTAL, HDIM, HDIM), jnp.float32)
    _, (attended, inflow) = lax.scan(forward_step, zero_state, (query_heads, key_heads, value_heads, log_prefix, log_total))
    flat_out = from_blocks(attended)
    grad_rows = grad_out.astype(jnp.float32)
    root_mean = jnp.sqrt(lax.optimization_barrier(jnp.mean(flat_out * flat_out, axis=-1, keepdims=True)) + epsilon)
    gain_term = lax.optimization_barrier(jnp.sum(grad_rows * flat_out / root_mean, axis=0))
    scaled = gain * grad_rows
    coefficient = lax.optimization_barrier(jnp.mean(scaled * flat_out, axis=-1, keepdims=True)) / root_mean ** 3
    grad_flat = scaled / root_mean - flat_out * coefficient
    grad_heads = grad_flat.reshape(N_CTX, TOK_DEV, HEAD_TOTAL, HDIM).transpose(0, 2, 1, 3)

    def backward_step(outflow, block_item):
        query_b, key_b, value_b, grad_b, prefix_b, total_b, inflow_b = block_item
        weights = decay_weights(prefix_b)
        score_masked = jnp.einsum('hte,hse->hts', query_b, key_b, precision=HIGHEST) * weights
        grad_masked = jnp.einsum('hte,hse->hts', grad_b, value_b, precision=HIGHEST) * weights
        growth = jnp.exp(prefix_b)[..., None]
        shrink = jnp.exp(total_b[:, None] - prefix_b)[..., None]
        grad_q = jnp.einsum('hts,hse->hte', grad_masked, key_b, precision=HIGHEST)
        grad_q = grad_q + growth * jnp.einsum('htf,hef->hte', grad_b, inflow_b, precision=HIGHEST)
        grad_k = jnp.einsum('hts,hte->hse', grad_masked, query_b, precision=HIGHEST)
        grad_k = grad_k + shrink * jnp.einsum('hef,hsf->hse', outflow, value_b, precision=HIGHEST)
        grad_v = jnp.einsum('hts,htf->hsf', score_masked, grad_b, precision=HIGHEST)
        grad_v = grad_v + shrink * jnp.einsum('hef,hse->hsf', outflow, key_b, precision=HIGHEST)
        local_part = jnp.einsum('hte,htf->hef', query_b * growth, grad_b, precision=HIGHEST)
        new_flow = local_part + jnp.exp(total_b)[:, None, None] * outflow
        return (new_flow, (grad_q, grad_k, grad_v))
    _, (grad_q, grad_k, grad_v) = lax.scan(backward_step, zero_state, (query_heads, key_heads, value_heads, grad_heads, log_prefix, log_total, inflow), reverse=True)
    return (from_blocks(grad_q).astype(jnp.bfloat16), from_blocks(grad_k).astype(jnp.bfloat16), from_blocks(grad_v).astype(jnp.bfloat16), gain_term)
```

```python
import functools

import jax
import jax.numpy as jnp
from jax import lax
from jax.experimental import pallas as pl
from jax.experimental.pallas import tpu as pltpu
from jax.sharding import PartitionSpec as P

F32 = jnp.float32
BF16 = jnp.bfloat16
MESH = pl.DeviceIdType.MESH
epsilon = 1e-06
TAIL = 8
LOG2E = 1.4426950408889634


def halves(x):
    high = x.astype(BF16)
    return high, (x - high.astype(F32)).astype(BF16)


def nn(a, b):
    return lax.dot_general(a, b, (((1,), (0,)), ((), ())), preferred_element_type=F32)


def nt(a, b):
    return lax.dot_general(a, b, (((1,), (1,)), ((), ())), preferred_element_type=F32)


def tn(a, b):
    return lax.dot_general(a, b, (((0,), (0,)), ((), ())), preferred_element_type=F32)


def beside(a, b):
    return jnp.concatenate([a, b], axis=1)


def above(a, b):
    return jnp.concatenate([a, b], axis=0)


class Chain:
    def __init__(self, shape, reverse, local, pair, total, others, prefix, back, flow, sems):
        self.n_ctx, self.heads, self.size, self.parts = shape
        self.local, self.pair, self.total, self.others = local, pair, total, others
        self.prefix, self.back, self.flow = prefix, back, flow
        self.pair_sems, self.back_sems, self.send_sems, self.recv_sems = sems
        me = lax.axis_index("ctx")
        self.z = lax.axis_index("fsdp")
        self.side = lax.rem(me, 2)
        self.group = me // 2
        self.partner = me + 1 - 2 * self.side
        self.half = self.heads // 2
        self.count = self.half // self.parts
        self.rounds = (self.n_ctx // 2).bit_length() - 1
        self.first = self.side == (1 if reverse else 0)
        self.late = []
        self.across = []
        for turn in range(self.rounds):
            bit = lax.rem(self.group // (1 << turn), 2)
            self.late.append(bit == (0 if reverse else 1))
            self.across.append((self.group + (1 << turn) * (1 - 2 * bit)) * 2 + self.side)

    def copy(self, src, dst, send, recv, ctx):
        return pltpu.make_async_remote_copy(
            src_ref=src, dst_ref=dst, send_sem=send, recv_sem=recv,
            device_id=(ctx, self.z), device_id_type=MESH,
        )

    def of_partner(self, i):
        return (1 - self.side) * self.half + i

    def of_mine(self, i):
        return self.side * self.half + i

    def at(self, part):
        return pl.ds(part * self.count, self.count)

    def pair_copy(self, part):
        return self.copy(
            self.local.at[pl.ds(self.of_partner(part * self.count), self.count)],
            self.pair.at[self.at(part)],
            self.pair_sems.at[0, part], self.pair_sems.at[1, part], self.partner,
        )

    def back_copy(self, part):
        return self.copy(
            self.back.at[self.at(part)],
            self.flow.at[pl.ds(self.of_mine(part * self.count), self.count)],
            self.back_sems.at[0, part], self.back_sems.at[1, part], self.partner,
        )

    def turn_copy(self, turn, part):
        return self.copy(
            self.total.at[turn, self.at(part)], self.others.at[turn, self.at(part)],
            self.send_sems.at[turn, part], self.recv_sems.at[turn, part], self.across[turn],
        )

    def turn_sends(self, turn, act):
        if turn < self.rounds - 1:
            act()
        else:
            pl.when(jnp.logical_not(self.late[turn]))(act)

    def ordered(self, i):
        mine = self.local[self.of_mine(i)]
        theirs = self.pair[i]
        return jnp.where(self.first, mine, theirs), jnp.where(self.first, theirs, mine)

    def join(self, early, late, into):
        size = self.size
        into[:size, :] = jnp.exp2(late[size : size + 1, :]) * early[:size] + late[:size]
        into[size:, :] = early[size:] + late[size:]

    def spread(self, part):
        self.pair_copy(part).wait()
        for n in range(self.count):
            i = part * self.count + n
            before, after = self.ordered(i)
            self.join(before, after, self.total.at[0, i])
            self.prefix[i] = jnp.zeros_like(before)
        self.turn_sends(0, lambda: self.turn_copy(0, part).start())

    def fold(self, turn, part):
        for n in range(self.count):
            i = part * self.count + n
            self.join(self.others[turn, i], self.prefix[i], self.prefix.at[i])

    def advance(self, turn, part):
        self.turn_copy(turn, part).wait_recv()
        for n in range(self.count):
            i = part * self.count + n
            mine, theirs = self.total[turn, i], self.others[turn, i]
            late = self.late[turn]
            early = jnp.where(late, theirs, mine)
            self.join(early, jnp.where(late, mine, theirs), self.total.at[turn + 1, i])
        self.turn_sends(turn + 1, lambda: self.turn_copy(turn + 1, part).start())
        pl.when(self.late[turn])(lambda: self.fold(turn, part))

    def close(self, part):
        last = self.rounds - 1

        @pl.when(self.late[last])
        def _():
            self.turn_copy(last, part).wait_recv()
            self.fold(last, part)

        size = self.size
        for n in range(self.count):
            i = part * self.count + n
            before, _ = self.ordered(i)
            early = self.prefix[i][:size]
            late = jnp.exp2(before[size : size + 1, :]) * early + before[:size]
            self.flow[self.of_mine(i)] = jnp.where(self.first, early, late)
            self.back[i] = jnp.where(self.first, late, early)
        self.back_copy(part).start()

    def drain(self):
        for turn in range(self.rounds):
            for part in range(self.parts):
                self.turn_sends(turn, lambda: self.turn_copy(turn, part).wait_send())


def kernel(
    sizes, q_in, k_in, v_in, go_in, log_ref, gain_ref,
    dq_ref, dk_ref, dv_ref, gg_ref, q_ref, k_ref, v_ref, go_ref, in_sems, block_sems,
    att, part_k, part_v, weights, turned_high, turned_low, squares, coupling, sums, gains, f_chunks, b_chunks, prefix_ref, columns,
    f_local, f_pair, f_total, f_others, f_prefix, f_back, f_flow,
    b_local, b_pair, b_total, b_others, b_prefix, b_back, b_flow,
    f_pair_sems, f_back_sems, f_send, f_recv,
    b_pair_sems, b_back_sems, b_send, b_recv,
    sum_send, sum_recv, gain_send, gain_recv,
):
    n_ctx, n_fsdp, rows, heads, size, chunk, parts, batch = sizes
    features = heads * size * n_fsdp
    half = heads // 2
    count = half // parts
    chunks = rows // chunk
    me, z = lax.axis_index("ctx"), lax.axis_index("fsdp")
    shape = (n_ctx, heads, size, parts)
    forward = Chain(
        shape, False, f_local, f_pair, f_total, f_others, f_prefix, f_back, f_flow,
        (f_pair_sems, f_back_sems, f_send, f_recv),
    )
    backward = Chain(
        shape, True, b_local, b_pair, b_total, b_others, b_prefix, b_back, b_flow,
        (b_pair_sems, b_back_sems, b_send, b_recv),
    )

    def block_loads(group):
        begin = group * batch * count
        for which, first in enumerate((forward.of_partner(begin), forward.of_mine(begin))):
            at = pl.ds(pl.multiple_of(first * size, size), batch * count * size)
            for n, (src, dst) in enumerate(((k_in, k_ref), (v_in, v_ref))):
                yield pltpu.make_async_copy(
                    src.at[:, at], dst.at[:, at], block_sems.at[group, 2 * which + n]
                )

    loads = [
        pltpu.make_async_copy(src, dst, in_sems.at[n])
        for n, (src, dst) in enumerate(((q_in, q_ref), (go_in, go_ref)))
    ]
    for group in range(parts // batch):
        for load in block_loads(group):
            load.start()
    for load in loads:
        load.start()

    barrier = pltpu.get_barrier_semaphore()
    for step in range(1, n_ctx):
        pl.semaphore_signal(
            barrier, inc=1, device_id=(lax.rem(me + step, n_ctx), z), device_id_type=MESH
        )
    for step in range(1, n_fsdp):
        pl.semaphore_signal(
            barrier, inc=1, device_id=(me, lax.rem(z + step, n_fsdp)), device_id_type=MESH
        )
    below = lax.broadcasted_iota(jnp.int32, (chunk, chunk), 0) >= lax.broadcasted_iota(
        jnp.int32, (chunk, chunk), 1
    )

    def lanes(head):
        return pl.ds(pl.multiple_of(head * size, size), size)

    class Decay:
        def __init__(self, head, first=False):
            self.head = head
            self.row = prefix_ref[pl.ds(head, 1), :]
            self.total = self.row[:, rows - 1 :]
            if first:
                columns[head] = jnp.broadcast_to(self.row, (size, rows)).T

        def column(self, c):
            return columns[self.head, span(c), :]

        def start(self, c):
            return self.row[:, c * chunk - 1 : c * chunk] if c else jnp.zeros((1, 1), F32)

        def end(self, c):
            return self.row[:, (c + 1) * chunk - 1 : (c + 1) * chunk]

        def growth(self, c):
            return jnp.exp2(self.column(c) - self.start(c))

        def shrink(self, c):
            return jnp.exp2(self.end(c) - self.column(c))

        def whole(self, c):
            return jnp.exp2(self.end(c) - self.start(c))

        def weight(self, c):
            return jnp.where(below, jnp.exp2(self.column(c) - self.row[:, span(c)]), 0.0)

    def span(c):
        return slice(c * chunk, (c + 1) * chunk)

    def loop(begin, end, body):
        lax.fori_loop(begin, end, lambda i, carry: (body(i), carry)[1], 0)

    def put_state(chain, head, state, total):
        chain.local[head, :size, :] = state
        chain.local[head, size:, :] = jnp.broadcast_to(total, (TAIL, size))

    def kv_state(head):
        decay = Decay(head, True)
        at = lanes(head)
        state = None
        for c in range(chunks):
            key, value = k_ref[span(c), at], v_ref[span(c), at]
            part = tn(above(key, key), above(*halves(value.astype(F32) * decay.shrink(c))))
            f_chunks[head * chunks + c] = part
            state = part if state is None else decay.whole(c) * state + part
        put_state(forward, head, state, decay.total)

    def attend(head):
        decay = Decay(head)
        at = lanes(head)
        flow = None
        for c in range(chunks):
            query, key, value = q_ref[span(c), at], k_ref[span(c), at], v_ref[span(c), at]
            weight = decay.weight(c)
            high, low = halves(nt(query, key) * weight)
            weights[head * chunks + c] = weight
            turned_high[head * chunks + c] = high.T
            turned_low[head * chunks + c] = low.T
            out = nn(beside(high, low), above(value, value))
            if flow is not None:
                out = out + decay.growth(c) * nn(beside(query, query), above(*halves(flow)))
            att[span(c), at] = out
            if c < chunks - 1:
                state = f_chunks[head * chunks + c]
                flow = state if flow is None else decay.whole(c) * flow + state

    def meet():
        pl.semaphore_wait(barrier, n_ctx - 1 + n_fsdp - 1)

    def run_states(chain, state, needs=lambda group: (), entry=None):
        def one(group):
            for load in needs(group):
                load.wait()
            mine = [group * batch + n for n in range(batch)]
            for part in mine:
                for n in range(count):
                    state(chain.of_partner(part * count + n))
                    state(chain.of_mine(part * count + n))
            if entry is not None:
                pl.when(group == 0)(entry)
            for part in mine:
                chain.pair_copy(part).start()

            @pl.when(group > 0)
            def _():
                for part in mine:
                    chain.spread(part - batch)

        loop(0, parts // batch, one)
        for n in range(batch):
            chain.spread(parts - batch + n)

    def run_cover(chain, body, pace):
        turns = chain.rounds - 1
        steps = half
        times, per = pace

        def one(i):
            body(2 * i)
            body(2 * i + 1)
            for turn in range(turns):
                for extra in range(-(-times // per)):
                    part = times * i // per + extra - turn * parts
                    end = jnp.minimum(times * (i + 1) // per - turn * parts, parts)

                    @pl.when((part >= 0) & (part < end))
                    def _():
                        chain.advance(turn, part)

        loop(0, steps, one)
        for turn in range(turns):
            done = min(max(times * steps // per - turn * parts, 0), parts)
            if done < parts:
                loop(done, parts, lambda part: chain.advance(turn, part))

    def run_flows(chain, body):
        def own(group):
            mine = [group * batch + n for n in range(batch)]
            for part in mine:
                chain.close(part)
            for part in mine:
                for n in range(count):
                    body(chain.of_mine(part * count + n))

        def other(group):
            mine = [group * batch + n for n in range(batch)]
            for part in mine:
                chain.back_copy(part).wait()
            for part in mine:
                for n in range(count):
                    body(chain.of_partner(part * count + n))

        loop(0, parts // batch, own)
        loop(0, parts // batch, other)

    logs = log_ref[...]
    high, rest = logs.astype(BF16), logs
    stacked = [high]
    for _ in range(2):
        rest = rest - high.astype(F32)
        high = rest.astype(BF16)
        stacked.append(high)
    upto = lax.broadcasted_iota(jnp.int32, (rows, rows), 0) <= lax.broadcasted_iota(
        jnp.int32, (rows, rows), 1
    )
    upto = jnp.where(upto, 1.0, 0.0).astype(BF16)
    prefix = nn(stacked[0], upto) + (nn(stacked[1], upto) + nn(stacked[2], upto))
    prefix_ref[...] = prefix * LOG2E
    run_states(forward, kv_state, block_loads, meet)
    loads[0].wait()
    run_cover(forward, attend, (1, 1))
    loads[1].wait()
    squares[...] = jnp.zeros_like(squares)
    coupling[...] = jnp.zeros_like(coupling)

    def inflow_in(head):
        decay = Decay(head)
        at = lanes(head)
        flow = above(*halves(f_flow[head]))
        gain_row = gain_ref[:, at]
        for c in range(chunks):
            query = q_ref[span(c), at]
            out = att[span(c), at] + jnp.exp2(decay.column(c)) * nn(beside(query, query), flow)
            att[span(c), at] = out
            squares[span(c), :] += out * out
            coupling[span(c), :] += gain_row * go_ref[span(c), at].astype(F32) * out

    run_flows(forward, inflow_in)

    which = lax.broadcasted_iota(jnp.int32, (TAIL, rows), 0)
    square_row = jnp.sum(squares[...].T, axis=0, keepdims=True)
    coupling_row = jnp.sum(coupling[...].T, axis=0, keepdims=True)
    sums[z] = jnp.where(which == 0, square_row, jnp.where(which == 1, coupling_row, 0.0))

    def sum_copy(step, slot):
        return pltpu.make_async_remote_copy(
            src_ref=sums.at[z], dst_ref=sums.at[slot],
            send_sem=sum_send.at[step - 1], recv_sem=sum_recv.at[slot],
            device_id=(me, lax.rem(z + step, n_fsdp)), device_id_type=MESH,
        )

    for step in range(1, n_fsdp):
        sum_copy(step, z).start()
    for step in range(1, n_fsdp):
        sum_copy(step, lax.rem(z + n_fsdp - step, n_fsdp)).wait_recv()
    both = sums[0]
    for slot in range(1, n_fsdp):
        both = both + sums[slot]
    both = both / features
    mean_square = jnp.broadcast_to(both[0:1, :], (size, rows)).T
    mean_coupling = jnp.broadcast_to(both[1:2, :], (size, rows)).T
    inverse = 1.0 / jnp.sqrt(mean_square + epsilon)
    squares[...] = inverse
    coupling[...] = mean_coupling * (inverse * inverse * inverse)

    def grad_state(head):
        decay = Decay(head)
        at = lanes(head)
        state = None
        gain_row = None
        for c in reversed(range(chunks)):
            grad = go_ref[span(c), at].astype(F32) * squares[span(c), :]
            out = att[span(c), at]
            term = jnp.sum(grad * out, axis=0, keepdims=True)
            gain_row = term if gain_row is None else gain_row + term
            grad = gain_ref[:, at] * grad - out * coupling[span(c), :]
            att[span(c), at] = grad
            query = q_ref[span(c), at]
            part = tn(above(query, query), above(*halves(grad * decay.growth(c))))
            b_chunks[head * chunks + c] = part
            state = part if state is None else decay.whole(c) * state + part
        gains[me, pl.ds(head, 1), :] = gain_row
        put_state(backward, head, state, decay.total)

    run_states(backward, grad_state)

    def gain_copy(step, slot):
        return pltpu.make_async_remote_copy(
            src_ref=gains.at[me], dst_ref=gains.at[slot],
            send_sem=gain_send.at[step - 1], recv_sem=gain_recv.at[slot],
            device_id=(lax.rem(me + step, n_ctx), z), device_id_type=MESH,
        )

    for step in range(1, n_ctx):
        gain_copy(step, me).start()

    def within(head):
        decay = Decay(head)
        at = lanes(head)
        outs = [None] * chunks
        for c in reversed(range(chunks - 1)):
            state = b_chunks[head * chunks + c + 1]
            later = outs[c + 1]
            outs[c] = state if later is None else decay.whole(c + 1) * later + state
        flow = f_flow[head]
        for c in range(chunks):
            query, key, value = q_ref[span(c), at], k_ref[span(c), at], v_ref[span(c), at]
            place = head * chunks + c
            grad = att[span(c), at]
            high, low = halves(grad)
            grad_high, grad_low = halves(
                nt(beside(high, low), beside(value, value)) * weights[place]
            )
            up_high, up_low = halves(grad * decay.growth(c))
            flow_high, flow_low = halves(flow)
            dq_ref[span(c), at] = (
                nn(beside(grad_high, grad_low), above(key, key))
                + nt(beside(up_high, up_low), beside(flow_high, flow_high))
                + nt(up_high, flow_low)
            ).astype(BF16)
            grad_k = tn(above(grad_high, grad_low), above(query, query))
            grad_v = nn(
                beside(turned_high[place], turned_low[place]), above(high, high)
            ) + nn(turned_high[place], low)
            if outs[c] is not None:
                shrink = decay.shrink(c)
                out_high, out_low = halves(outs[c])
                grad_k = grad_k + shrink * nt(beside(value, value), beside(out_high, out_low))
                grad_v = grad_v + shrink * nn(beside(key, key), above(out_high, out_low))
            if c < chunks - 1:
                flow = decay.whole(c) * flow + f_chunks[place]
            part_k[span(c), at] = grad_k
            part_v[span(c), at] = grad_v

    run_cover(backward, within, (3, 2))

    def outflow_in(head):
        decay = Decay(head)
        at = lanes(head)
        high, low = halves(b_flow[head])
        for c in range(chunks):
            shrink = jnp.exp2(decay.total - decay.column(c))
            key, value = k_ref[span(c), at], v_ref[span(c), at]
            into_k = nt(beside(value, value), beside(high, low))
            into_v = nn(beside(key, key), above(high, low))
            dk_ref[span(c), at] = (part_k[span(c), at] + shrink * into_k).astype(BF16)
            dv_ref[span(c), at] = (part_v[span(c), at] + shrink * into_v).astype(BF16)

    run_flows(backward, outflow_in)
    forward.drain()
    backward.drain()

    for step in range(1, n_ctx):
        gain_copy(step, lax.rem(me + n_ctx - step, n_ctx)).wait_recv()
    total = gains[0]
    for slot in range(1, n_ctx):
        total = total + gains[slot]
    for head in range(heads):
        gg_ref[:, head * size : (head + 1) * size] = total[head : head + 1]
    for step in range(1, n_fsdp):
        sum_copy(step, z).wait_send()
    for step in range(1, n_ctx):
        gain_copy(step, me).wait_send()


def shards(queries, keys, values, grad_out, log_decay, gain):
    n_ctx, n_fsdp = lax.axis_size("ctx"), lax.axis_size("fsdp")
    rows, heads = log_decay.shape
    size = queries.shape[1] // heads
    chunk = size
    assert rows % chunk == 0
    half, rounds = heads // 2, (n_ctx // 2).bit_length() - 1
    parts = half
    batch = 2 if parts % 2 == 0 else 1
    vmem = pl.BlockSpec(memory_space=pltpu.VMEM)
    hbm = pl.BlockSpec(memory_space=pl.ANY)
    out = jax.ShapeDtypeStruct(queries.shape, BF16)
    held = pltpu.VMEM(queries.shape, BF16)
    chain = [
        pltpu.VMEM((heads, size + TAIL, size), F32),
        pltpu.VMEM((half, size + TAIL, size), F32),
        pltpu.VMEM((rounds, half, size + TAIL, size), F32),
        pltpu.VMEM((rounds, half, size + TAIL, size), F32),
        pltpu.VMEM((half, size + TAIL, size), F32),
        pltpu.VMEM((half, size, size), F32),
        pltpu.VMEM((heads, size, size), F32),
    ]
    dma = pltpu.SemaphoreType.DMA
    chain_sems = [dma((2, parts)), dma((2, parts)), dma((rounds, parts)), dma((rounds, parts))]
    grad_q, grad_k, grad_v, grad_gain = pl.pallas_call(
        functools.partial(kernel, (n_ctx, n_fsdp, rows, heads, size, chunk, parts, batch)),
        out_shape=[held, held, held, jax.ShapeDtypeStruct((1, heads * size), F32)],
        in_specs=[hbm] * 4 + [vmem] * 2,
        out_specs=[vmem] * 4,
        scratch_shapes=[pltpu.VMEM(queries.shape, BF16)] * 4
        + [dma((2,)), dma((parts // batch, 4))]
        + [pltpu.VMEM(queries.shape, F32)] * 3
        + [pltpu.VMEM((heads * (rows // chunk), chunk, chunk), F32)]
        + [pltpu.VMEM((heads * (rows // chunk), chunk, chunk), BF16)] * 2
        + [pltpu.VMEM((rows, size), F32)] * 2
        + [pltpu.VMEM((n_fsdp, TAIL, rows), F32), pltpu.VMEM((n_ctx, heads, size), F32)]
        + [pltpu.VMEM((heads * (rows // chunk), size, size), F32)] * 2
        + [pltpu.VMEM((heads, rows), F32), pltpu.VMEM((heads, rows, size), F32)]
        + chain + chain + chain_sems + chain_sems
        + [dma((max(n_fsdp - 1, 1),)), dma((n_fsdp,)), dma((n_ctx - 1,)), dma((n_ctx,))],
        compiler_params=pltpu.CompilerParams(
            collective_id=0, has_side_effects=True, vmem_limit_bytes=56 << 20,
        ),
    )(queries, keys, values, grad_out, log_decay.T, gain.reshape(1, -1))
    return grad_q, grad_k, grad_v, grad_gain.reshape(-1)


def solution(mesh):
    return jax.shard_map(
        shards,
        mesh=mesh,
        in_specs=(P("ctx", "fsdp"),) * 5 + (P("fsdp"),),
        out_specs=(P("ctx", "fsdp"), P("ctx", "fsdp"), P("ctx", "fsdp"), P("fsdp")),
        check_vma=False,
    )
```

```python
import functools

import jax
import jax.numpy as jnp
from jax import lax
from jax.experimental import pallas as pl
from jax.experimental.pallas import tpu as pltpu
from jax.sharding import PartitionSpec as P

F32 = jnp.float32
BF16 = jnp.bfloat16
MESH = pl.DeviceIdType.MESH
epsilon = 1e-06
TAIL = 8
LOG2E = 1.4426950408889634


def halves(x):
    high = x.astype(BF16)
    return high, (x - high.astype(F32)).astype(BF16)


def nn(a, b):
    return lax.dot_general(a, b, (((1,), (0,)), ((), ())), preferred_element_type=F32)


def nt(a, b):
    return lax.dot_general(a, b, (((1,), (1,)), ((), ())), preferred_element_type=F32)


def tn(a, b):
    return lax.dot_general(a, b, (((0,), (0,)), ((), ())), preferred_element_type=F32)


def beside(a, b):
    return jnp.concatenate([a, b], axis=1)


def above(a, b):
    return jnp.concatenate([a, b], axis=0)


class Chain:
    def __init__(self, shape, reverse, local, pair, total, others, prefix, back, flow, sems):
        self.n_ctx, self.heads, self.size, self.parts = shape
        self.local, self.pair, self.total, self.others = local, pair, total, others
        self.prefix, self.back, self.flow = prefix, back, flow
        self.pair_sems, self.back_sems, self.send_sems, self.recv_sems = sems
        me = lax.axis_index("ctx")
        self.z = lax.axis_index("fsdp")
        self.side = lax.rem(me, 2)
        self.group = me // 2
        self.partner = me + 1 - 2 * self.side
        self.half = self.heads // 2
        self.count = self.half // self.parts
        self.rounds = (self.n_ctx // 2).bit_length() - 1
        self.first = self.side == (1 if reverse else 0)
        self.late = []
        self.across = []
        for turn in range(self.rounds):
            bit = lax.rem(self.group // (1 << turn), 2)
            self.late.append(bit == (0 if reverse else 1))
            self.across.append((self.group + (1 << turn) * (1 - 2 * bit)) * 2 + self.side)

    def copy(self, src, dst, send, recv, ctx):
        return pltpu.make_async_remote_copy(
            src_ref=src, dst_ref=dst, send_sem=send, recv_sem=recv,
            device_id=(ctx, self.z), device_id_type=MESH,
        )

    def of_partner(self, i):
        return (1 - self.side) * self.half + i

    def of_mine(self, i):
        return self.side * self.half + i

    def at(self, part):
        return pl.ds(part * self.count, self.count)

    def pair_copy(self, part):
        return self.copy(
            self.local.at[pl.ds(self.of_partner(part * self.count), self.count)],
            self.pair.at[self.at(part)],
            self.pair_sems.at[0, part], self.pair_sems.at[1, part], self.partner,
        )

    def back_copy(self, part):
        return self.copy(
            self.back.at[self.at(part)],
            self.flow.at[pl.ds(self.of_mine(part * self.count), self.count)],
            self.back_sems.at[0, part], self.back_sems.at[1, part], self.partner,
        )

    def turn_copy(self, turn, part):
        return self.copy(
            self.total.at[turn, self.at(part)], self.others.at[turn, self.at(part)],
            self.send_sems.at[turn, part], self.recv_sems.at[turn, part], self.across[turn],
        )

    def turn_sends(self, turn, act):
        if turn < self.rounds - 1:
            act()
        else:
            pl.when(jnp.logical_not(self.late[turn]))(act)

    def ordered(self, i):
        mine = self.local[self.of_mine(i)]
        theirs = self.pair[i]
        return jnp.where(self.first, mine, theirs), jnp.where(self.first, theirs, mine)

    def join(self, early, late, into):
        size = self.size
        into[:size, :] = jnp.exp2(late[size : size + 1, :]) * early[:size] + late[:size]
        into[size:, :] = early[size:] + late[size:]

    def spread(self, part):
        self.pair_copy(part).wait()
        for n in range(self.count):
            i = part * self.count + n
            before, after = self.ordered(i)
            self.join(before, after, self.total.at[0, i])
            self.prefix[i] = jnp.zeros_like(before)
        self.turn_sends(0, lambda: self.turn_copy(0, part).start())

    def fold(self, turn, part):
        for n in range(self.count):
            i = part * self.count + n
            self.join(self.others[turn, i], self.prefix[i], self.prefix.at[i])

    def advance(self, turn, part):
        self.turn_copy(turn, part).wait_recv()
        for n in range(self.count):
            i = part * self.count + n
            mine, theirs = self.total[turn, i], self.others[turn, i]
            late = self.late[turn]
            early = jnp.where(late, theirs, mine)
            self.join(early, jnp.where(late, mine, theirs), self.total.at[turn + 1, i])
        self.turn_sends(turn + 1, lambda: self.turn_copy(turn + 1, part).start())
        pl.when(self.late[turn])(lambda: self.fold(turn, part))

    def close(self, part):
        last = self.rounds - 1

        @pl.when(self.late[last])
        def _():
            self.turn_copy(last, part).wait_recv()
            self.fold(last, part)

        size = self.size
        for n in range(self.count):
            i = part * self.count + n
            before, _ = self.ordered(i)
            early = self.prefix[i][:size]
            late = jnp.exp2(before[size : size + 1, :]) * early + before[:size]
            self.flow[self.of_mine(i)] = jnp.where(self.first, early, late)
            self.back[i] = jnp.where(self.first, late, early)
        self.back_copy(part).start()

    def drain(self):
        for turn in range(self.rounds):
            for part in range(self.parts):
                self.turn_sends(turn, lambda: self.turn_copy(turn, part).wait_send())


def kernel(
    sizes, q_in, k_in, v_in, go_in, log_ref, gain_ref,
    dq_ref, dk_ref, dv_ref, gg_ref, q_ref, k_ref, v_ref, go_ref, in_sems, block_sems,
    att, part_k, part_v, weights, turned_high, turned_low, squares, coupling, sums, gains, f_chunks, b_chunks, prefix_ref, columns,
    f_local, f_pair, f_total, f_others, f_prefix, f_back, f_flow,
    b_local, b_pair, b_total, b_others, b_prefix, b_back, b_flow,
    f_pair_sems, f_back_sems, f_send, f_recv,
    b_pair_sems, b_back_sems, b_send, b_recv,
    sum_send, sum_recv, gain_send, gain_recv,
):
    n_ctx, n_fsdp, rows, heads, size, chunk, parts, batch = sizes
    features = heads * size * n_fsdp
    half = heads // 2
    count = half // parts
    chunks = rows // chunk
    me, z = lax.axis_index("ctx"), lax.axis_index("fsdp")
    shape = (n_ctx, heads, size, parts)
    forward = Chain(
        shape, False, f_local, f_pair, f_total, f_others, f_prefix, f_back, f_flow,
        (f_pair_sems, f_back_sems, f_send, f_recv),
    )
    backward = Chain(
        shape, True, b_local, b_pair, b_total, b_others, b_prefix, b_back, b_flow,
        (b_pair_sems, b_back_sems, b_send, b_recv),
    )

    def block_loads(group):
        begin = group * batch * count
        for which, first in enumerate((forward.of_partner(begin), forward.of_mine(begin))):
            at = pl.ds(pl.multiple_of(first * size, size), batch * count * size)
            for n, (src, dst) in enumerate(((k_in, k_ref), (v_in, v_ref))):
                yield pltpu.make_async_copy(
                    src.at[:, at], dst.at[:, at], block_sems.at[group, 2 * which + n]
                )

    loads = [
        pltpu.make_async_copy(src, dst, in_sems.at[n])
        for n, (src, dst) in enumerate(((q_in, q_ref), (go_in, go_ref)))
    ]
    for group in range(parts // batch):
        for load in block_loads(group):
            load.start()
    for load in loads:
        load.start()

    barrier = pltpu.get_barrier_semaphore()
    for step in range(1, n_ctx):
        pl.semaphore_signal(
            barrier, inc=1, device_id=(lax.rem(me + step, n_ctx), z), device_id_type=MESH
        )
    for step in range(1, n_fsdp):
        pl.semaphore_signal(
            barrier, inc=1, device_id=(me, lax.rem(z + step, n_fsdp)), device_id_type=MESH
        )
    below = lax.broadcasted_iota(jnp.int32, (chunk, chunk), 0) >= lax.broadcasted_iota(
        jnp.int32, (chunk, chunk), 1
    )

    def lanes(head):
        return pl.ds(pl.multiple_of(head * size, size), size)

    class Decay:
        def __init__(self, head, first=False):
            self.head = head
            self.row = prefix_ref[pl.ds(head, 1), :]
            self.total = self.row[:, rows - 1 :]
            if first:
                columns[head] = jnp.broadcast_to(self.row, (size, rows)).T

        def column(self, c):
            return columns[self.head, span(c), :]

        def start(self, c):
            return self.row[:, c * chunk - 1 : c * chunk] if c else jnp.zeros((1, 1), F32)

        def end(self, c):
            return self.row[:, (c + 1) * chunk - 1 : (c + 1) * chunk]

        def growth(self, c):
            return jnp.exp2(self.column(c) - self.start(c))

        def shrink(self, c):
            return jnp.exp2(self.end(c) - self.column(c))

        def whole(self, c):
            return jnp.exp2(self.end(c) - self.start(c))

        def weight(self, c):
            return jnp.where(below, jnp.exp2(self.column(c) - self.row[:, span(c)]), 0.0)

    def span(c):
        return slice(c * chunk, (c + 1) * chunk)

    def loop(begin, end, body):
        lax.fori_loop(begin, end, lambda i, carry: (body(i), carry)[1], 0)

    def put_state(chain, head, state, total):
        chain.local[head, :size, :] = state
        chain.local[head, size:, :] = jnp.broadcast_to(total, (TAIL, size))

    def kv_state(head):
        decay = Decay(head, True)
        at = lanes(head)
        state = None
        for c in range(chunks):
            key, value = k_ref[span(c), at], v_ref[span(c), at]
            part = tn(above(key, key), above(*halves(value.astype(F32) * decay.shrink(c))))
            f_chunks[head * chunks + c] = part
            state = part if state is None else decay.whole(c) * state + part
        put_state(forward, head, state, decay.total)

    def attend(head):
        decay = Decay(head)
        at = lanes(head)
        flow = None
        for c in range(chunks):
            query, key, value = q_ref[span(c), at], k_ref[span(c), at], v_ref[span(c), at]
            weight = decay.weight(c)
            high, low = halves(nt(query, key) * weight)
            weights[head * chunks + c] = weight
            turned_high[head * chunks + c] = high.T
            turned_low[head * chunks + c] = low.T
            out = nn(beside(high, low), above(value, value))
            if flow is not None:
                out = out + decay.growth(c) * nn(beside(query, query), above(*halves(flow)))
            att[span(c), at] = out
            if c < chunks - 1:
                state = f_chunks[head * chunks + c]
                flow = state if flow is None else decay.whole(c) * flow + state

    def meet():
        pl.semaphore_wait(barrier, n_ctx - 1 + n_fsdp - 1)

    def run_states(chain, state, needs=lambda group: (), entry=None):
        def one(group):
            for load in needs(group):
                load.wait()
            mine = [group * batch + n for n in range(batch)]
            for part in mine:
                for n in range(count):
                    state(chain.of_partner(part * count + n))
                    state(chain.of_mine(part * count + n))
            if entry is not None:
                pl.when(group == 0)(entry)
            for part in mine:
                chain.pair_copy(part).start()

            @pl.when(group > 0)
            def _():
                for part in mine:
                    chain.spread(part - batch)

        loop(0, parts // batch, one)
        for n in range(batch):
            chain.spread(parts - batch + n)

    def run_cover(chain, body, pace):
        turns = chain.rounds - 1
        steps = half
        times, per = pace

        def one(i):
            body(2 * i)
            body(2 * i + 1)
            for turn in range(turns):
                for extra in range(-(-times // per)):
                    part = times * i // per + extra - turn * parts
                    end = jnp.minimum(times * (i + 1) // per - turn * parts, parts)

                    @pl.when((part >= 0) & (part < end))
                    def _():
                        chain.advance(turn, part)

        loop(0, steps, one)
        for turn in range(turns):
            done = min(max(times * steps // per - turn * parts, 0), parts)
            if done < parts:
                loop(done, parts, lambda part: chain.advance(turn, part))

    def run_flows(chain, body):
        def own(group):
            mine = [group * batch + n for n in range(batch)]
            for part in mine:
                chain.close(part)
            for part in mine:
                for n in range(count):
                    body(chain.of_mine(part * count + n))

        def other(group):
            mine = [group * batch + n for n in range(batch)]
            for part in mine:
                chain.back_copy(part).wait()
            for part in mine:
                for n in range(count):
                    body(chain.of_partner(part * count + n))

        loop(0, parts // batch, own)
        loop(0, parts // batch, other)

    logs = log_ref[...]
    high, rest = logs.astype(BF16), logs
    stacked = [high]
    for _ in range(2):
        rest = rest - high.astype(F32)
        high = rest.astype(BF16)
        stacked.append(high)
    upto = lax.broadcasted_iota(jnp.int32, (rows, rows), 0) <= lax.broadcasted_iota(
        jnp.int32, (rows, rows), 1
    )
    upto = jnp.where(upto, 1.0, 0.0).astype(BF16)
    prefix = nn(stacked[0], upto) + (nn(stacked[1], upto) + nn(stacked[2], upto))
    prefix_ref[...] = prefix * LOG2E
    run_states(forward, kv_state, block_loads, meet)
    loads[0].wait()
    run_cover(forward, attend, (1, 1))
    loads[1].wait()
    squares[...] = jnp.zeros_like(squares)
    coupling[...] = jnp.zeros_like(coupling)

    def inflow_in(head):
        decay = Decay(head)
        at = lanes(head)
        flow = above(*halves(f_flow[head]))
        gain_row = gain_ref[:, at]
        for c in range(chunks):
            query = q_ref[span(c), at]
            out = att[span(c), at] + jnp.exp2(decay.column(c)) * nn(beside(query, query), flow)
            att[span(c), at] = out
            squares[span(c), :] += out * out
            coupling[span(c), :] += gain_row * go_ref[span(c), at].astype(F32) * out

    run_flows(forward, inflow_in)

    which = lax.broadcasted_iota(jnp.int32, (TAIL, rows), 0)
    square_row = jnp.sum(squares[...].T, axis=0, keepdims=True)
    coupling_row = jnp.sum(coupling[...].T, axis=0, keepdims=True)
    sums[z] = jnp.where(which == 0, square_row, jnp.where(which == 1, coupling_row, 0.0))

    def sum_copy(step, slot):
        return pltpu.make_async_remote_copy(
            src_ref=sums.at[z], dst_ref=sums.at[slot],
            send_sem=sum_send.at[step - 1], recv_sem=sum_recv.at[slot],
            device_id=(me, lax.rem(z + step, n_fsdp)), device_id_type=MESH,
        )

    for step in range(1, n_fsdp):
        sum_copy(step, z).start()
    for step in range(1, n_fsdp):
        sum_copy(step, lax.rem(z + n_fsdp - step, n_fsdp)).wait_recv()
    both = sums[0]
    for slot in range(1, n_fsdp):
        both = both + sums[slot]
    both = both / features
    mean_square = jnp.broadcast_to(both[0:1, :], (size, rows)).T
    mean_coupling = jnp.broadcast_to(both[1:2, :], (size, rows)).T
    inverse = 1.0 / jnp.sqrt(mean_square + epsilon)
    squares[...] = inverse
    coupling[...] = mean_coupling * (inverse * inverse * inverse)

    def grad_state(head):
        decay = Decay(head)
        at = lanes(head)
        state = None
        gain_row = None
        for c in reversed(range(chunks)):
            grad = go_ref[span(c), at].astype(F32) * squares[span(c), :]
            out = att[span(c), at]
            term = jnp.sum(grad * out, axis=0, keepdims=True)
            gain_row = term if gain_row is None else gain_row + term
            grad = gain_ref[:, at] * grad - out * coupling[span(c), :]
            att[span(c), at] = grad
            query = q_ref[span(c), at]
            part = tn(above(query, query), above(*halves(grad * decay.growth(c))))
            b_chunks[head * chunks + c] = part
            state = part if state is None else decay.whole(c) * state + part
        gains[me, pl.ds(head, 1), :] = gain_row
        put_state(backward, head, state, decay.total)

    run_states(backward, grad_state)

    def gain_copy(step, slot):
        return pltpu.make_async_remote_copy(
            src_ref=gains.at[me], dst_ref=gains.at[slot],
            send_sem=gain_send.at[step - 1], recv_sem=gain_recv.at[slot],
            device_id=(lax.rem(me + step, n_ctx), z), device_id_type=MESH,
        )

    for step in range(1, n_ctx):
        gain_copy(step, me).start()

    def within(head):
        decay = Decay(head)
        at = lanes(head)
        outs = [None] * chunks
        for c in reversed(range(chunks - 1)):
            state = b_chunks[head * chunks + c + 1]
            later = outs[c + 1]
            outs[c] = state if later is None else decay.whole(c + 1) * later + state
        flow = f_flow[head]
        for c in range(chunks):
            query, key, value = q_ref[span(c), at], k_ref[span(c), at], v_ref[span(c), at]
            place = head * chunks + c
            grad = att[span(c), at]
            high, low = halves(grad)
            grad_high, grad_low = halves(
                nt(beside(high, low), beside(value, value)) * weights[place]
            )
            up_high, up_low = halves(grad * decay.growth(c))
            flow_high, flow_low = halves(flow)
            dq_ref[span(c), at] = (
                nn(beside(grad_high, grad_low), above(key, key))
                + nt(beside(up_high, up_low), beside(flow_high, flow_high))
                + nt(up_high, flow_low)
            ).astype(BF16)
            grad_k = tn(above(grad_high, grad_low), above(query, query))
            grad_v = nn(
                beside(turned_high[place], turned_low[place]), above(high, high)
            ) + nn(turned_high[place], low)
            if outs[c] is not None:
                shrink = decay.shrink(c)
                out_high, out_low = halves(outs[c])
                grad_k = grad_k + shrink * nt(beside(value, value), beside(out_high, out_low))
                grad_v = grad_v + shrink * nn(beside(key, key), above(out_high, out_low))
            if c < chunks - 1:
                flow = decay.whole(c) * flow + f_chunks[place]
            part_k[span(c), at] = grad_k
            part_v[span(c), at] = grad_v

    run_cover(backward, within, (3, 2))

    def outflow_in(head):
        decay = Decay(head)
        at = lanes(head)
        high, low = halves(b_flow[head])
        for c in range(chunks):
            shrink = jnp.exp2(decay.total - decay.column(c))
            key, value = k_ref[span(c), at], v_ref[span(c), at]
            into_k = nt(beside(value, value), beside(high, low))
            into_v = nn(beside(key, key), above(high, low))
            dk_ref[span(c), at] = (part_k[span(c), at] + shrink * into_k).astype(BF16)
            dv_ref[span(c), at] = (part_v[span(c), at] + shrink * into_v).astype(BF16)

    run_flows(backward, outflow_in)
    forward.drain()
    backward.drain()

    for step in range(1, n_ctx):
        gain_copy(step, lax.rem(me + n_ctx - step, n_ctx)).wait_recv()
    total = gains[0]
    for slot in range(1, n_ctx):
        total = total + gains[slot]
    for head in range(heads):
        gg_ref[:, head * size : (head + 1) * size] = total[head : head + 1]
    for step in range(1, n_fsdp):
        sum_copy(step, z).wait_send()
    for step in range(1, n_ctx):
        gain_copy(step, me).wait_send()


def flush(*refs):
    count = len(refs) // 2
    sems = refs[-1]
    copies = [
        pltpu.make_async_copy(refs[n], refs[count + n], sems.at[n]) for n in range(count)
    ]
    for copy in copies:
        copy.start()
    for copy in copies:
        copy.wait()


def shards(queries, keys, values, grad_out, log_decay, gain):
    n_ctx, n_fsdp = lax.axis_size("ctx"), lax.axis_size("fsdp")
    rows, heads = log_decay.shape
    size = queries.shape[1] // heads
    chunk = size
    assert rows % chunk == 0
    half, rounds = heads // 2, (n_ctx // 2).bit_length() - 1
    parts = half
    batch = 2 if parts % 2 == 0 else 1
    vmem = pl.BlockSpec(memory_space=pltpu.VMEM)
    hbm = pl.BlockSpec(memory_space=pl.ANY)
    out = jax.ShapeDtypeStruct(queries.shape, BF16)
    held = pltpu.VMEM(queries.shape, BF16)
    chain = [
        pltpu.VMEM((heads, size + TAIL, size), F32),
        pltpu.VMEM((half, size + TAIL, size), F32),
        pltpu.VMEM((rounds, half, size + TAIL, size), F32),
        pltpu.VMEM((rounds, half, size + TAIL, size), F32),
        pltpu.VMEM((half, size + TAIL, size), F32),
        pltpu.VMEM((half, size, size), F32),
        pltpu.VMEM((heads, size, size), F32),
    ]
    dma = pltpu.SemaphoreType.DMA
    chain_sems = [dma((2, parts)), dma((2, parts)), dma((rounds, parts)), dma((rounds, parts))]
    results = pl.pallas_call(
        functools.partial(kernel, (n_ctx, n_fsdp, rows, heads, size, chunk, parts, batch)),
        out_shape=[held, held, held, pltpu.VMEM((1, heads * size), F32)],
        in_specs=[hbm] * 4 + [vmem] * 2,
        out_specs=[vmem] * 4,
        scratch_shapes=[pltpu.VMEM(queries.shape, BF16)] * 4
        + [dma((2,)), dma((parts // batch, 4))]
        + [pltpu.VMEM(queries.shape, F32)] * 3
        + [pltpu.VMEM((heads * (rows // chunk), chunk, chunk), F32)]
        + [pltpu.VMEM((heads * (rows // chunk), chunk, chunk), BF16)] * 2
        + [pltpu.VMEM((rows, size), F32)] * 2
        + [pltpu.VMEM((n_fsdp, TAIL, rows), F32), pltpu.VMEM((n_ctx, heads, size), F32)]
        + [pltpu.VMEM((heads * (rows // chunk), size, size), F32)] * 2
        + [pltpu.VMEM((heads, rows), F32), pltpu.VMEM((heads, rows, size), F32)]
        + chain + chain + chain_sems + chain_sems
        + [dma((max(n_fsdp - 1, 1),)), dma((n_fsdp,)), dma((n_ctx - 1,)), dma((n_ctx,))],
        compiler_params=pltpu.CompilerParams(
            collective_id=0, has_side_effects=True, vmem_limit_bytes=56 << 20,
        ),
    )(queries, keys, values, grad_out, log_decay.T, gain.reshape(1, -1))
    row = jax.ShapeDtypeStruct((1, heads * size), F32)
    grad_q, grad_k, grad_v, grad_gain = pl.pallas_call(
        flush,
        out_shape=[out, out, out, row],
        in_specs=[hbm] * 4,
        out_specs=[hbm] * 4,
        scratch_shapes=[dma((4,))],
        compiler_params=pltpu.CompilerParams(vmem_limit_bytes=1 << 20),
    )(*results)
    return grad_q, grad_k, grad_v, grad_gain.reshape(-1)


def solution(mesh):
    return jax.shard_map(
        shards,
        mesh=mesh,
        in_specs=(P("ctx", "fsdp"),) * 5 + (P("fsdp"),),
        out_specs=(P("ctx", "fsdp"), P("ctx", "fsdp"), P("ctx", "fsdp"), P("fsdp")),
        check_vma=False,
    )
```
